32 devices in a mesh: tm: 4 (over z), gx: 2 (over y), gy: 4 (over x, core).
Axes of the slice: x: 2, y: 2, z: 4, core: 2. Of those that a mesh axis runs over, the one named last changes fastest.
Arguments:
- segment_opening_values: float32 [4, 4, 24, 64, 128], P('tm', None, 'gx', 'gy'), may hold values from -6 to 6
- cell_material_label: int32 [24, 64, 128], P('gx', 'gy'), may hold values from 0 to 5
- material_rigidity: float32 [6], replicated, may hold values from 0.3 to 3
- dilation_mismatch: float32 [6], replicated, may hold values from -1 to 1
- heat_swings_array: float32 [4, 2], P('tm'), may hold values from 0.5 to 4
- prony_coefficients: float32 [3], replicated, may hold values from 0.2 to 2
- prony_decay_times: float32 [3], replicated, may hold values from 0.7 to 48
Outputs:
- end_state: float32 [4, 4, 24, 64, 128], P('tm', None, 'gx', 'gy')
The draws below stay inside these ranges and needn't reach their ends.
All inputs are finite; a program needn't handle non-finite values.
Results may differ from the reference program's by a relative error of at most 0.0001.
Values sent between devices are 32-bit elements; how exact they have to be, the bound alone decides.
A program may use at most 64 MiB of HBM per device.

```python
import math
import jax
import jax.numpy as jnp

PRONY = 3
REGIONS = 6
PARTITION_PACES = 2
SHARP_SOLVER_ITER = 3
LOOSE_SOLVER_ITER = 2
STATE = 4
NX = 24
NY = 64
NZ = 128
N_TM = 4


def with_ends(drawn, rng, least, top_value):
    shape = drawn.shape
    place = [jax.random.randint(jax.random.fold_in(rng, axis), (), 0, shape[axis]) for axis in range(len(shape))]
    drawn = drawn.at[tuple(place)].set(least)
    longest = shape.index(max(shape))
    place[longest] = (place[longest] + 1) % shape[longest]
    return drawn.at[tuple(place)].set(top_value)


def level_of(stream_key, extent, pieces, low, high):
    factor_of, own = 1.0, jax.random.fold_in(stream_key, 6)
    for dim, blocks in pieces:
        steps = jnp.exp(jax.random.uniform(jax.random.fold_in(own, dim), (blocks,), jnp.float32, low / len(pieces), high / len(pieces)))
        factor_of = factor_of * jnp.repeat(steps, extent[dim] // blocks).reshape([-1 if axis == dim else 1 for axis in range(len(extent))])
    return factor_of


def normal_values(stream_key, extent, scale, bound, shards=(), held_as=jnp.bfloat16):
    drawn = scale * jax.random.normal(stream_key, extent, jnp.float32)
    if shards:
        drawn = drawn * level_of(stream_key, extent, shards, -0.22, 0.18)
    return jnp.clip(drawn, -bound, bound).astype(held_as)


def setup_inputs(seed: int = 0) -> dict:
    streams_of = jax.random.split(jax.random.key(seed), 8)
    return {
        "segment_opening_values": normal_values(streams_of[0], (N_TM, STATE, NX, NY, NZ), 1.0, 6.0, ((0, 4), (2, 2), (3, 4)), jnp.float32),
        "cell_material_label": with_ends(jax.random.randint(streams_of[1], (NX, NY, NZ), 0, REGIONS), jax.random.fold_in(streams_of[1], 1), 0, REGIONS - 1).astype(jnp.int32),
        "material_rigidity": jnp.clip(jnp.exp(jax.random.uniform(streams_of[2], (REGIONS,), jnp.float32, math.log(0.3), math.log(3.0))), 0.3, 3.0),
        "dilation_mismatch": jnp.clip(jax.random.uniform(streams_of[3], (REGIONS,), jnp.float32, -1.0, 1.0), -1.0, 1.0),
        "heat_swings_array": jnp.clip(0.5 + 3.5 * jax.random.uniform(streams_of[4], (N_TM, PARTITION_PACES), jnp.float32) ** level_of(streams_of[4], (N_TM, PARTITION_PACES), ((0, 4),), -0.2, 0.2), 0.5, 4.0),
        "prony_coefficients": jnp.clip(jnp.exp(jax.random.uniform(streams_of[5], (PRONY,), jnp.float32, math.log(0.2), math.log(2.0))), 0.2, 2.0),
        "prony_decay_times": jnp.clip(jnp.exp(jax.random.uniform(streams_of[6], (PRONY,), jnp.float32, math.log(0.7), math.log(48.0))), 0.7, 48.0),
    }


corners = [(near_one, near_two, near_three) for near_one in (0, 1) for near_two in (0, 1) for near_three in (0, 1)]
diagonal_weights = [1.0 / 3.0] * 8
thermal_weights = [0.25 * (2 * near_three - 1) for near_one, near_two, near_three in corners]


def region_lookup(cell_material_label, region_table):
    looked_up = jnp.zeros(cell_material_label.shape, region_table.dtype)
    for region in range(region_table.shape[0]):
        looked_up = looked_up + jnp.where(cell_material_label == region, region_table[region], jnp.zeros((), region_table.dtype))
    return looked_up


def stencil_apply(padded, cell_rigidity):
    extent_one, extent_two, extent_three = cell_rigidity.shape
    values = [padded[near_one:near_one + extent_one, near_two:near_two + extent_two, near_three:near_three + extent_three] for near_one, near_two, near_three in corners]
    corner_total = values[0]
    for corner_value in values[1:]:
        corner_total = corner_total + corner_value
    result = None
    for corner_index, (near_one, near_two, near_three) in enumerate(corners):
        face_sum = values[corner_index ^ 4] + values[corner_index ^ 2] + values[corner_index ^ 1]
        element_part = cell_rigidity * ((5.0 / 12.0) * values[corner_index] + (face_sum - corner_total) / 12.0)
        node_part = element_part[1 - near_one:extent_one - near_one, 1 - near_two:extent_two - near_two, 1 - near_three:extent_three - near_three]
        result = node_part if result is None else result + node_part
    return result


def nodal_sum(element_field, weights):
    extent_one, extent_two, extent_three = element_field.shape
    result = None
    for corner_index, (near_one, near_two, near_three) in enumerate(corners):
        node_part = weights[corner_index] * element_field[1 - near_one:extent_one - near_one, 1 - near_two:extent_two - near_two, 1 - near_three:extent_three - near_three]
        result = node_part if result is None else result + node_part
    return result


def apply_operator(field, shift_value, cell_rigidity):
    return shift_value * field + stencil_apply(jnp.pad(field, 1), cell_rigidity)


def conjugate_solve(rhs_field, initial, shift_value, diagonal, cell_rigidity, iterations):
    solution = initial
    remainder = rhs_field - apply_operator(solution, shift_value, cell_rigidity)
    scaled = remainder / diagonal
    search = scaled
    gamma_now = jnp.sum(remainder * scaled)
    for iteration in range(iterations):
        image = apply_operator(search, shift_value, cell_rigidity)
        step_size = gamma_now / jnp.sum(search * image)
        solution = solution + step_size * search
        if iteration + 1 < iterations:
            remainder = remainder - step_size * image
            scaled = remainder / diagonal
            gamma_next = jnp.sum(remainder * scaled)
            search = scaled + (gamma_next / gamma_now) * search
            gamma_now = gamma_next
    return solution


def moment_forward(present_displacements, heat_level, step_length, iterations, dilation_deformation, rigidity_main_terms, cell_rigidity, prony_coefficients, prony_decay_times):
    decay_rate = jnp.exp(-step_length / prony_decay_times)
    factors = prony_coefficients * decay_rate
    shift_value = 1.0 / step_length + jnp.sum(factors)
    history = present_displacements[1:]
    rhs_field = present_displacements[0] / step_length + heat_level * dilation_deformation + jnp.sum(factors[:, None, None, None] * history, axis=0)
    displaced = conjugate_solve(rhs_field, present_displacements[0], shift_value, shift_value + rigidity_main_terms, cell_rigidity, iterations)
    history = decay_rate[:, None, None, None] * history + (1.0 - decay_rate)[:, None, None, None] * displaced[None]
    return jnp.concatenate([displaced[None], history], axis=0)


def reference(segment_opening_values, cell_material_label, material_rigidity, dilation_mismatch, heat_swings_array, prony_coefficients, prony_decay_times):
    coefficient = region_lookup(cell_material_label, material_rigidity)
    loaded = coefficient * region_lookup(cell_material_label, dilation_mismatch)
    cell_rigidity = jnp.pad(coefficient, ((1, 0), (1, 0), (1, 0)))
    element_load = jnp.pad(loaded, ((1, 0), (1, 0), (1, 0)))
    dilation_deformation = nodal_sum(element_load, thermal_weights)
    rigidity_main_terms = nodal_sum(cell_rigidity, diagonal_weights)
    loose_interval_span = 1.0 * PARTITION_PACES
    corrections = []
    first_coarse = None
    for segment_number in range(N_TM):
        present_displacements = segment_opening_values[segment_number]
        for sharp_interval_span in range(PARTITION_PACES):
            present_displacements = moment_forward(present_displacements, heat_swings_array[segment_number, sharp_interval_span], 1.0, SHARP_SOLVER_ITER, dilation_deformation, rigidity_main_terms, cell_rigidity, prony_coefficients, prony_decay_times)
        crude_advance_operator = moment_forward(segment_opening_values[segment_number], heat_swings_array[segment_number, PARTITION_PACES - 1], loose_interval_span, LOOSE_SOLVER_ITER, dilation_deformation, rigidity_main_terms, cell_rigidity, prony_coefficients, prony_decay_times)
        corrections.append(present_displacements - crude_advance_operator)
        if segment_number == 0:
            first_coarse = crude_advance_operator
    segment_closing_values = []
    for segment_number in range(N_TM):
        if segment_number == 0:
            crude_prediction = first_coarse
        else:
            crude_prediction = moment_forward(segment_closing_values[-1], heat_swings_array[segment_number, PARTITION_PACES - 1], loose_interval_span, LOOSE_SOLVER_ITER, dilation_deformation, rigidity_main_terms, cell_rigidity, prony_coefficients, prony_decay_times)
        segment_closing_values.append(crude_prediction + corrections[segment_number])
    return jnp.stack(segment_closing_values)
```

```python
import functools

import jax
import jax.numpy as jnp
from jax import lax
from jax.experimental import pallas as pl
from jax.experimental.pallas import tpu as pltpu
from jax.sharding import PartitionSpec as P

PARTITION_PACES = 2
SHARP_SOLVER_ITER = 3
LOOSE_SOLVER_ITER = 2
MESH = pl.DeviceIdType.MESH
F32 = jnp.float32
PAD = 8
SIDE = 4
CHUNKS = 3

MF, ML = SHARP_SOLVER_ITER, LOOSE_SOLVER_ITER
RIM = MF + 1
LAB, U0, H1, HD, HC, HIST = range(6)
R_FINE1, R_COARSE, R_FINE2, R_STAGE = range(4)


def chunks_of(nx):
    cut = [nx * j // CHUNKS for j in range(CHUNKS + 1)]
    return [(a, b - a) for a, b in zip(cut, cut[1:]) if b > a]


def loop(count, body, carry=0, unroll=True):
    return lax.fori_loop(0, count, body, carry, unroll=unroll)


def kernel(
    sizes,
    state,
    labels,
    rigidity,
    mismatch,
    heat,
    coefs,
    times,
    out,
    lab_x,
    in_x,
    k_b,
    kal_b,
    kz_b,
    cx_b,
    cy_b,
    cz_b,
    s8_b,
    theta_b,
    ef_b,
    el_b,
    vf,
    vg,
    vc,
    vs,
    xf,
    xg,
    xs,
    ab,
    au_b,
    rb_b,
    u_b,
    aa_b,
    hb,
    own_ab,
    gu_out,
    gu_in,
    y_out,
    y_in,
    first_in,
    heat_out,
    heat_in,
    part,
    red,
    halo_send,
    halo_recv,
    red_send,
    red_recv,
    z_send,
    z_recv,
    y_send,
    y_recv,
    heat_send,
    heat_recv,
    token,
):
    n_tm, n_gx, n_gy = sizes
    _, prony, nx, ny, nz = state.shape
    prony -= 1
    h = RIM
    wide = ny + 2 * PAD
    span_y = ny + 2 * SIDE
    stages = n_tm - 1
    inner = max(stages - 1, 0)
    tm, gx, gy = lax.axis_index("tm"), lax.axis_index("gx"), lax.axis_index("gy")
    me = gx * n_gy + gy
    n_peer = n_gx * n_gy
    own_r, own_c = pl.ds(h, nx), pl.ds(PAD, ny)
    XF = HIST + prony
    XG = XF + MF
    XS = XG + MF
    AB = XS + ML * inner
    first_plane = tm == 0
    chunks = chunks_of(nx)

    def win(ref, e, shift=0):
        return ref[e, pl.ds(SIDE + shift, span_y)]

    def put(ref, e, value):
        ref[e, pl.ds(SIDE, span_y)] = value

    directions = [(a, b) for a in (-1, 0, 1) for b in (-1, 0, 1) if (a, b) != (0, 0)]
    compass = directions + [(0, 0)]

    def exists(a, b):
        return (gx + a >= 0) & (gx + a < n_gx) & (gy + b >= 0) & (gy + b < n_gy)

    lab_x[...] = jnp.full(lab_x.shape, -1, jnp.int32)

    barrier = pltpu.get_barrier_semaphore()

    def greet(t, a, b):
        pl.semaphore_signal(barrier, inc=1, device_id=(t, a, b), device_id_type=MESH)

    for j in range(1, n_peer):
        peer = lax.rem(me + j, n_peer)
        greet(tm, peer // n_gy, lax.rem(peer, n_gy))

    for step in (-1, 1):

        @pl.when((tm + step >= 0) & (tm + step < n_tm))
        def _():
            greet(tm + step, gx, gy)

    def count_of(flag):
        return jnp.where(flag, 1, 0).astype(jnp.int32)

    cross = count_of(tm > 0) + count_of(tm < n_tm - 1)

    def splat(value):
        return jnp.full((1, nz), value, F32)

    def decays(dt):
        decay = [jnp.exp(-dt / splat(times[p])) for p in range(prony)]
        factor = [splat(coefs[p]) * decay[p] for p in range(prony)]
        return decay, factor

    fine_dt, loose_dt = 1.0, 1.0 * PARTITION_PACES
    d_f, f_f = decays(fine_dt)
    d_l, f_l = decays(loose_dt)
    s_f = sum(f_f, splat(1.0 / fine_dt))
    s_l = sum(f_l, splat(1.0 / loose_dt))
    keep_f = [1.0 - d for d in d_f]
    keep_l = [1.0 - d for d in d_l]
    prods = range(prony)
    held = sum((f_f[p] * d_f[p] for p in prods), splat(0.0))
    kappa_f = sum((f_l[p] * keep_f[p] for p in prods), splat(0.0))
    kappa_l = sum((f_l[p] * keep_l[p] for p in prods), splat(0.0))
    gain_f = 1.0 / fine_dt - s_f
    gain_l = 1.0 / loose_dt - s_l
    heat_f = [splat(heat[0, s]) for s in range(PARTITION_PACES)]
    heat_l = heat_f[PARTITION_PACES - 1]

    def fill(i, carry):
        lab_x[h + i, own_c] = labels[i]
        hist = [state[0, 1 + p, i] for p in prods]
        in_x[U0 - 1, h + i, own_c] = state[0, 0, i]
        in_x[H1 - 1, h + i, own_c] = sum(f_f[p] * hist[p] for p in prods)
        in_x[HD - 1, h + i, own_c] = sum((f_f[p] * d_f[p]) * hist[p] for p in prods)
        in_x[HC - 1, h + i, own_c] = sum(f_l[p] * hist[p] for p in prods)
        for p in prods:
            in_x[HIST - 1 + p, h + i, own_c] = hist[p]
        return carry

    def clear_strips(refs, value, dtype):
        row = jnp.full((wide, nz), value, dtype)
        pad = jnp.full((PAD, nz), value, dtype)
        for flag, start in ((gx == 0, 0), (gx == n_gx - 1, h + nx)):

            @pl.when(flag)
            def _():
                for ref in refs:
                    for i in range(h):
                        ref[start + i] = row

        for flag, start in ((gy == 0, 0), (gy == n_gy - 1, PAD + ny)):

            @pl.when(flag)
            def _():
                def body(i, carry):
                    for ref in refs:
                        ref[i, pl.ds(start, PAD)] = pad
                    return carry

                lax.fori_loop(0, nx + 2 * h, body, 0)

    loop(nx, fill, unroll=4)
    pl.semaphore_wait(barrier, n_peer - 1 + cross)

    def src_r(a, w):
        return {-1: pl.ds(h, w), 0: own_r, 1: pl.ds(h + nx - w, w)}[a]

    def dst_r(a, w):
        return {-1: pl.ds(h + nx, w), 0: own_r, 1: pl.ds(h - w, w)}[a]

    src_c = {-1: pl.ds(PAD, SIDE), 0: own_c, 1: pl.ds(PAD + ny - SIDE, SIDE)}
    dst_c = {-1: pl.ds(PAD + ny, SIDE), 0: own_c, 1: pl.ds(PAD - SIDE, SIDE)}

    def halo_copy(ref, which, rim, index):
        a, b = directions[index]
        return pltpu.make_async_remote_copy(
            src_ref=ref.at[src_r(a, rim), src_c[b]],
            dst_ref=ref.at[dst_r(a, rim), dst_c[b]],
            send_sem=halo_send.at[which, index],
            recv_sem=halo_recv.at[which, index],
            device_id=(tm, gx + a, gy + b),
            device_id_type=MESH,
        )

    def halo_each(messages, sign, act):
        for index, (a, b) in enumerate(directions):

            @pl.when(exists(sign * a, sign * b))
            def _():
                for ref, which, rim in messages:
                    act(halo_copy(ref, which, rim, index))

    def halo_start(*messages):
        halo_each(messages, 1, lambda c: c.start())

    def halo_wait(*messages):
        halo_each(messages, -1, lambda c: c.wait_recv())

    def halo_drain(*messages):
        halo_each(messages, 1, lambda c: c.wait_send())

    def field(which, rim):
        return (lab_x if which == LAB else in_x.at[which - 1], which, rim)

    m_lab, m_u0, m_h1 = field(LAB, RIM), field(U0, RIM), field(H1, MF)
    m_hd, m_hc = field(HD, MF), field(HC, ML)
    m_hist = [field(HIST + p, ML) for p in prods]
    m_xf = [(xf.at[k], XF + k, MF) for k in range(MF)]
    m_xg = [(xg.at[k], XG + k, ML) for k in range(MF)]

    def m_xs(n):
        base = ML * (n - 1)
        return [(xs.at[base + k], XS + base + k, ML) for k in range(ML)]

    def give_copy(n, f, index):
        a, b = compass[index]
        w = ML + 1
        rows = {-1: pl.ds(0, w), 0: pl.ds(0, nx), 1: pl.ds(nx - w, w)}[a]
        cols = {-1: pl.ds(0, SIDE), 0: pl.ds(0, ny), 1: pl.ds(ny - SIDE, SIDE)}[b]
        at = 2 * (n - 1) + f
        return pltpu.make_async_remote_copy(
            src_ref=own_ab.at[f, rows, cols],
            dst_ref=ab.at[at, dst_r(a, w), dst_c[b]],
            send_sem=halo_send.at[AB + at, index],
            recv_sem=halo_recv.at[AB + at, index],
            device_id=(tm - n, gx + a, gy + b),
            device_id_type=MESH,
        )

    def give_each(n, f, sign, act):
        for index, (a, b) in enumerate(compass):

            @pl.when(exists(sign * a, sign * b))
            def _():
                act(give_copy(n, f, index))

    def give(f, act):
        for n in range(1, stages):
            for index, (a, b) in enumerate(compass):

                @pl.when((tm == n) & exists(a, b))
                def _():
                    act(give_copy(n, f, index))

    def heat_copy():
        return pltpu.make_async_remote_copy(
            src_ref=heat_out,
            dst_ref=heat_in,
            send_sem=heat_send,
            recv_sem=heat_recv,
            device_id=(tm - 1, gx, gy),
            device_id_type=MESH,
        )

    def z_items(j):
        if j < stages:
            return [(j - 1, pl.ds(0, nx))]
        return [(stages - 1 + k, pl.ds(*cut)) for k, cut in enumerate(chunks)]

    def z_copies(j, n):
        return [
            pltpu.make_async_remote_copy(
                src_ref=gu_out.at[j - 1, at],
                dst_ref=gu_in.at[j - 1, at],
                send_sem=z_send.at[n - 1, item],
                recv_sem=z_recv.at[item],
                device_id=(tm + n, gx, gy),
                device_id_type=MESH,
            )
            for item, at in z_items(j)
        ]

    def up_copy(item, first):
        if item >= prony:
            src, dst = own_ab.at[item - prony], first_in.at[item - prony]
        else:
            src = state.at[0, 1 + item] if first else y_out.at[item]
            dst = y_in.at[item]
        return pltpu.make_async_remote_copy(
            src_ref=src,
            dst_ref=dst,
            send_sem=y_send.at[item],
            recv_sem=y_recv.at[item],
            device_id=(tm + 1, gx, gy),
            device_id_type=MESH,
        )

    halo_start(m_lab)
    halo_start(m_u0)
    halo_start(m_h1)
    halo_start(m_hd)

    @pl.when(first_plane)
    def _():
        for p in prods:
            up_copy(p, True).start()
        if inner:
            pl.semaphore_signal(
                token, inc=1, device_id=(tm + 1, gx, gy), device_id_type=MESH
            )

    @pl.when(tm > 0)
    def _():
        halo_start(m_hc)

    def heat_relay():
        heat_copy().wait_recv()
        heat_out[...] = heat_in[...]
        heat_out[tm - 1] = jnp.broadcast_to(heat_l, (8, nz))
        heat_copy().start()

    @pl.when(tm == n_tm - 1)
    def _():
        heat_out[...] = jnp.zeros(heat_out.shape, F32)
        heat_out[tm - 1] = jnp.broadcast_to(heat_l, (8, nz))
        heat_copy().start()

    clear_strips([in_x.at[j] for j in range(4 + prony)], 0.0, F32)

    def red_copy(which, j):
        peer = lax.rem(me + j, n_peer)
        return pltpu.make_async_remote_copy(
            src_ref=part.at[which],
            dst_ref=red.at[which, n_peer - 1 - j],
            send_sem=red_send.at[which],
            recv_sem=red_recv.at[which],
            device_id=(tm, peer // n_gy, lax.rem(peer, n_gy)),
            device_id_type=MESH,
        )

    def red_all(which):
        return pltpu.make_async_remote_copy(
            src_ref=red.at[which],
            dst_ref=red.at[which],
            send_sem=red_send.at[which],
            recv_sem=red_recv.at[which],
            device_id=(tm, gx, gy),
            device_id_type=MESH,
        )

    def red_start(which, sums):
        for j, value in enumerate(sums):
            part[which, j : j + 1] = jnp.sum(value, axis=0, keepdims=True)
        for j in range(1, n_peer):
            red_copy(which, j).start()

    def red_finish(which, count):
        if n_peer > 1:
            red_all(which).wait_recv()
        values = [part[which]] + [red[which, j] for j in range(n_peer - 1)]
        while len(values) > 1:
            values = [
                values[i] + values[i + 1] if i + 1 < len(values) else values[i]
                for i in range(0, len(values), 2)
            ]
        total = jnp.broadcast_to(
            jnp.sum(values[0], axis=1, keepdims=True), values[0].shape
        )
        return [total[j : j + 1] for j in range(count)]

    def red_drain(which):
        if n_peer > 1:
            red_all(which).wait_send()

    lane = lax.broadcasted_iota(jnp.int32, (span_y, nz), 1)
    first_lane, last_lane = lane == 0, lane == nz - 1

    def next_z(v):
        return pltpu.roll(v, nz - 1, 1)

    def prior_z(v):
        return jnp.where(first_lane, 0.0, pltpu.roll(v, 1, 1))

    def prior_y(v):
        return v + pltpu.roll(v, 1, 0)

    def span(margin):
        if n_gx == 1:
            return h, nx
        if n_gx == 2:
            return h - margin * gx, nx + margin
        return h - margin, nx + 2 * margin

    def apply(src, emit, margin):
        low, count = span(margin)

        def load(e):
            c = win(src, e)
            return c, next_z(c)

        def box(c, up):
            d = c + jnp.where(last_lane, 0.0, up)
            return d + pltpu.roll(d, span_y - 1, 0)

        before, before_up = load(low - 1)
        here, here_up = load(low)
        after, after_up = load(low + 1)
        box_b, box_h = box(before, before_up), box(here, here_up)
        g = win(k_b, low - 1) * (box_b + box_h)
        q = win(cx_b, low - 1) * before

        def body(t, carry):
            g_b, q_b, c, up, bx, c1, up1 = carry
            e = low + t
            c2, up2 = load(e + 2)
            bx1 = box(c1, up1)
            g = win(k_b, e) * (bx + bx1)
            gy_ = prior_y(g + g_b)
            cx, cz = win(cx_b, e), win(cz_b, e)
            t0 = (
                win(s8_b, e) * c
                + win(cy_b, e) * win(src, e, 1)
                + win(cy_b, e, -1) * win(src, e, -1)
                + cz * up
                + (cx * c1 + q_b)
                - gy_
            )
            emit(e, c, t0 + prior_z(cz * c - gy_))
            return g, cx * c, c1, up1, bx1, c2, up2

        loop(count, body, (g, q, here, here_up, box_h, after, after_up))

    def over(margin, body, unroll=True):
        low, count = span(margin)

        def step(t, carry):
            body(low + t)
            return carry

        loop(count, step, unroll=unroll)

    def own_copy(dst, src):
        def body(i, carry):
            dst[h + i, own_c] = src[h + i, own_c]
            return carry

        loop(nx, body)

    def moments(v, m, shift):
        zero = jnp.zeros((ny, nz), F32)

        def body(i, sums):
            diag = shift + 4.0 * s8_b[h + i, own_c]
            x = [v[k][h + i, own_c] for k in range(m + 1)]
            got = []
            for k in range(m):
                weighted = diag * x[k]
                got += [weighted * x[k], weighted * x[k + 1]]
            return tuple(s + g for s, g in zip(sums, got))

        return loop(nx, body, (zero,) * (2 * m))

    def krylov(v, m, inv_b, which, shift, after=None):
        for k in range(m):

            def emit(e, c, t):
                put(v[k + 1], e, win(inv_b, e) * t)

            apply(v[k], emit, m - 1 - k)
            if after is not None and k + 1 < m:
                after(k)
        red_start(which, moments(v, m, shift))
        if after is not None:
            after(m - 1)

    def galerkin(nu, m):
        a = [nu[j] + nu[j + 1] for j in range(2 * m - 1)]
        lower = [[None] * m for _ in range(m)]
        inverse, y = [], []
        for i in range(m):
            row = []
            for j in range(i):
                value = a[i + j]
                for q in range(j):
                    value = value - row[q] * lower[j][q]
                row.append(value)
                lower[i][j] = value * inverse[j]
            pivot, rhs = a[2 * i], nu[i]
            for q in range(i):
                pivot = pivot - row[q] * lower[i][q]
                rhs = rhs - lower[i][q] * y[q]
            good = pivot > 0.0
            inverse.append(jnp.where(good, 1.0 / jnp.where(good, pivot, 1.0), 0.0))
            y.append(rhs)
        c = [None] * m
        for i in reversed(range(m)):
            value = y[i] * inverse[i]
            for q in range(i + 1, m):
                value = value - lower[q][i] * c[q]
            c[i] = value
        return c

    def spread(values, n=None):
        n = span_y if n is None else n
        return [jnp.broadcast_to(v, (n, nz)) for v in values]

    def combine(c, x):
        m = len(c)
        w = c[0] * x[0]
        for k in range(1, m):
            w = w + c[k] * x[k]
        both = [c[0]] + [c[k - 1] + c[k] for k in range(1, m)] + [c[m - 1]]
        sh = both[0] * x[0]
        for k in range(1, m + 1):
            sh = sh + both[k] * x[k]
        return w, sh

    zero_row = jnp.zeros((wide, nz), F32)
    sources = [v.at[k] for v in (vf, vg) for k in range(MF)]
    sources += [vc.at[k] for k in range(ML)]
    sources += [vs.at[(ML + 1) * n + k] for n in range(stages) for k in range(ML)]
    for ref in sources:
        ref[h - 1] = zero_row
        ref[h + nx] = zero_row
    clear_strips(
        [xf.at[k] for k in range(MF)]
        + [xg.at[k] for k in range(MF)]
        + [xs.at[k] for k in range(ML * inner)]
        + [ab.at[k] for k in range(2 * inner)],
        0.0,
        F32,
    )
    regions = rigidity.shape[0]
    kel_of = [rigidity[r] * (1.0 / 12.0) for r in range(regions)]
    kal_of = [kel_of[r] * mismatch[r] for r in range(regions)]
    wide_lane = lax.broadcasted_iota(jnp.int32, (wide, nz), 1)
    node_y = gy * ny - PAD + SIDE + lax.broadcasted_iota(jnp.int32, (span_y, nz), 0)
    inside_y = (node_y >= 0) & (node_y < n_gy * ny)

    halo_wait(m_lab)
    low_e, count_e = span(MF)

    def lookup(e):
        ids = lab_x[e]
        kel = jnp.zeros((wide, nz), F32)
        kal = jnp.zeros((wide, nz), F32)
        for region in range(regions):
            here = ids == region
            kel = jnp.where(here, kel_of[region], kel)
            kal = jnp.where(here, kal_of[region], kal)
        k_b[e] = kel
        kal_b[e] = kal
        kz_b[e] = kel + jnp.where(wide_lane == 0, 0.0, pltpu.roll(kel, 1, 1))

    def nodal(e):
        kz = win(kz_b, e)
        kyz = kz + win(kz_b, e, -1)
        ky = win(k_b, e) + win(k_b, e, -1)
        kal = win(kal_b, e) + win(kal_b, e, -1)
        put(cx_b, e, kyz)
        return kyz, kz, ky, prior_z(kal) - kal

    lookup(low_e - 1)
    lookup(low_e)

    def setup(t, carry):
        e = low_e + t
        lookup(e)
        new = nodal(e)
        s8 = carry[0] + new[0]
        put(s8_b, e, s8)
        put(cy_b, e, carry[1] + new[1])
        put(cz_b, e, jnp.where(last_lane, 0.0, carry[2] + new[2]))
        put(theta_b, e, 3.0 * (carry[3] + new[3]))
        node_x = gx * nx - h + e
        inside = inside_y & (node_x >= 0) & (node_x < n_gx * nx)
        diag = 4.0 * s8
        put(ef_b, e, jnp.where(inside, 1.0 / (s_f + diag), 0.0))
        put(el_b, e, jnp.where(inside, 1.0 / (s_l + diag), 0.0))
        return new

    loop(count_e, setup, nodal(low_e - 1))

    @pl.when((tm > 0) & (tm == n_tm - 2))
    def _():
        heat_relay()

    u0_x, h1_x = in_x.at[U0 - 1], in_x.at[H1 - 1]
    hist_x = [in_x.at[HIST - 1 + p] for p in prods]
    halo_wait(m_u0, m_h1)

    def first_level(e, c, t):
        image = t + 4.0 * win(s8_b, e) * c
        put(au_b, e, image)
        r = gain_f * c + heat_f[0] * win(theta_b, e) + win(h1_x, e) - image
        put(vf.at[0], e, win(ef_b, e) * r)

    apply(u0_x, first_level, MF)

    def sender(x, v, messages):
        def after(k):
            own_copy(x.at[k], v[k + 1])
            halo_start(messages[k])

        return after

    vf_ = [vf.at[k] for k in range(MF + 1)]
    vg_ = [vg.at[k] for k in range(MF + 1)]
    vc_ = [vc.at[k] for k in range(ML + 1)]
    xf_ = [vf.at[0]] + [xf.at[k] for k in range(MF)]
    xg_ = [vg.at[0]] + [xg.at[k] for k in range(MF)]
    krylov(vf_, MF, ef_b, R_FINE1, s_f, sender(xf, vf_, m_xf))

    halo_wait(m_hd)
    hd_x, hc_x = in_x.at[HD - 1], in_x.at[HC - 1]

    def base_fine2(e):
        r = heat_f[1] * win(theta_b, e) - held * win(u0_x, e) - win(au_b, e)
        put(rb_b, e, r + win(hd_x, e))

    over(MF, base_fine2)

    @pl.when(first_plane)
    def _():
        halo_start(*m_hist)

    @pl.when((tm > 0) & (tm < n_tm - 2))
    def _():
        heat_relay()

    if inner:

        @pl.when((tm > 0) & (tm < stages))
        def _():
            pl.semaphore_wait(token, 1)

        @pl.when((tm > 0) & (tm < stages - 1))
        def _():
            pl.semaphore_signal(
                token, inc=1, device_id=(tm + 1, gx, gy), device_id_type=MESH
            )

    @pl.when(tm > 0)
    def _():
        halo_wait(m_hc)

        def coarse_first(e):
            r = gain_l * win(u0_x, e) + heat_l * win(theta_b, e) - win(au_b, e)
            r = r + win(hc_x, e)
            put(vc.at[0], e, win(el_b, e) * r)

        over(ML, coarse_first)
        krylov(vc_, ML, el_b, R_COARSE, s_l)

    c1 = galerkin(red_finish(R_FINE1, 2 * MF), MF)
    c1w = spread(c1)
    halo_wait(*m_xf)
    lift_f = s_f - held

    def second_level(e):
        w, sh = combine(c1w, [win(x, e) for x in xf_])
        put(vg.at[0], e, win(ef_b, e) * (win(rb_b, e) + lift_f * w) - sh)

    over(MF, second_level)

    @pl.when(first_plane)
    def _():
        krylov(vg_, MF, ef_b, R_FINE2, s_f, sender(xg, vg_, m_xg))

        def after_fine1(e):
            w, sh = combine(c1w, [win(x, e) for x in xf_])
            u = win(u0_x, e) + w
            image = win(au_b, e) + (s_f + 4.0 * win(s8_b, e)) * sh - s_f * w
            put(u_b, e, u)
            put(au_b, e, image)
            r = (gain_l + kappa_f) * u - image
            for p in prods:
                past = d_l[p] * win(hist_x[p], e) + (d_f[p] * keep_f[p]) * u
                put(hb.at[p], e, past)
                r = r + f_l[p] * past
            put(rb_b, e, r)

        halo_wait(*m_hist)
        over(ML, after_fine1)

        def keep_u1(i, carry):
            own_ab[1, i] = u_b[h + i, own_c]
            return carry

        loop(nx, keep_u1)
        up_copy(prony + 1, True).start()
        heat_copy().wait_recv()

        def add_heat(e):
            put(rb_b, e, win(rb_b, e) + heat_in[0, 0:1] * win(theta_b, e))

        over(ML, add_heat)

        c2w = spread(galerkin(red_finish(R_FINE2, 2 * MF), MF))
        halo_wait(*m_xg)
        lift = gain_l + kappa_f + s_f

        def v_of(n):
            return [vs.at[(ML + 1) * (n - 1) + k] for k in range(ML + 1)]

        def x_of(n):
            return [v_of(n)[0]] + [xs.at[ML * (n - 1) + k] for k in range(ML)]

        def stage_start(n):
            v = v_of(n)
            after = None
            if n < stages:
                after = sender(xs.at[pl.ds(ML * (n - 1), ML)], v, m_xs(n))
            krylov(v, ML, el_b, R_STAGE + n - 1, s_l, after)

        def stage1_level(e):
            w, sh = combine(c2w, [win(x, e) for x in xg_])
            r = win(rb_b, e) + lift * w - (s_f + 4.0 * win(s8_b, e)) * sh
            put(v_of(1)[0], e, win(el_b, e) * r)

        over(ML, stage1_level)
        stage_start(1)

        def after_fine2(e):
            w, sh = combine(c2w, [win(x, e) for x in xg_])
            u = win(u_b, e) + w
            put(u_b, e, u)
            image = win(au_b, e) + (s_f + 4.0 * win(s8_b, e)) * sh - s_f * w
            put(au_b, e, image)
            for p in prods:
                put(hb.at[p], e, win(hb.at[p], e) + keep_f[p] * u)

        over(ML, after_fine2)

        def first_out(i, carry):
            u = u_b[h + i, own_c]
            own_ab[0, i] = u
            out[0, 0, i] = u
            for p in prods:
                out[0, 1 + p, i] = hb[p, h + i, own_c]
            return carry

        loop(nx, first_out)
        up_copy(prony, True).start()

        rise = gain_l + kappa_l + s_l
        for n in range(1, stages):
            a_x, b_x = ab.at[2 * (n - 1)], ab.at[2 * (n - 1) + 1]
            give_each(n, 1, -1, lambda c: c.wait_recv())
            give_each(n, 0, -1, lambda c: c.wait_recv())

            def correction(e, c, t):
                put(aa_b, e, t + 4.0 * win(s8_b, e) * c)

            apply(a_x, correction, ML)

            def base_stage(e):
                a, b, u = win(a_x, e), win(b_x, e), win(u_b, e)
                r = gain_l * (u + a) - win(au_b, e) - win(aa_b, e)
                r = r + kappa_l * u + kappa_f * a
                r = r + heat_in[n, 0:1] * win(theta_b, e)
                for p in prods:
                    past = d_l[p] * win(hb.at[p], e) + (d_f[p] * keep_f[p]) * b
                    r = r + f_l[p] * past
                put(rb_b, e, r)

            over(ML, base_stage)
            cw = spread(galerkin(red_finish(R_STAGE + n - 1, 2 * ML), ML))
            halo_wait(*m_xs(n))

            def stage_level(e):
                w, sh = combine(cw, [win(x, e) for x in x_of(n)])
                r = win(rb_b, e) + rise * w
                put(v_of(n + 1)[0], e, win(el_b, e) * r - sh)

            over(ML, stage_level)
            stage_start(n + 1)

            def after_stage(e):
                w, sh = combine(cw, [win(x, e) for x in x_of(n)])
                moved = win(u_b, e) + w
                a, b = win(a_x, e), win(b_x, e)
                put(u_b, e, moved + a)
                image = win(au_b, e) + (s_l + 4.0 * win(s8_b, e)) * sh - s_l * w
                put(au_b, e, image + win(aa_b, e))
                for p in prods:
                    past = d_l[p] * win(hb.at[p], e) + keep_l[p] * moved
                    put(hb.at[p], e, past + keep_f[p] * (a + d_f[p] * b))

            over(ML, after_stage)

            def stage_out(i, carry):
                gu_out[n - 1, i] = u_b[h + i, own_c] - a_x[h + i, own_c]
                return carry

            loop(nx, stage_out)
            for to in range(n, n_tm):
                for copy in z_copies(n, to):
                    copy.start()

        v = v_of(stages)
        c = galerkin(red_finish(R_STAGE + stages - 1, 2 * ML), ML)
        cw = spread(c, ny)
        for index, (start, count) in enumerate(chunks):

            def last_stage(i, carry):
                e = h + start + i
                u = u_b[e, own_c]
                for k in range(ML):
                    u = u + cw[k] * v[k][e, own_c]
                gu_out[stages - 1, start + i] = u
                return carry

            loop(count, last_stage)
            z_copies(stages, stages)[index].start()

        halo_drain(*m_xg)
        for n in range(1, stages):
            halo_drain(*m_xs(n))
        for n in range(stages):
            red_drain(R_STAGE + n)
        for j in range(1, n_tm):
            for to in range(j, n_tm):
                for copy in z_copies(j, to):
                    copy.wait_send()
        for item in range(prony + 2):
            up_copy(item, True).wait_send()
        halo_drain(*m_hist)

    @pl.when(tm > 0)
    def _():
        krylov(vg_, MF, ef_b, R_FINE2, s_f)
        c1o = spread(c1, ny)
        cco = spread(galerkin(red_finish(R_COARSE, 2 * ML), ML), ny)

        def early(i, carry):
            e = h + i
            b = c1o[0] * vf[0, e, own_c]
            for k in range(1, MF):
                b = b + c1o[k] * vf[k, e, own_c]
            for k in range(ML):
                b = b - cco[k] * vc[k, e, own_c]
            own_ab[1, i] = b
            return carry

        loop(nx, early)
        give(1, lambda c: c.start())

        c2o = spread(galerkin(red_finish(R_FINE2, 2 * MF), MF), ny)

        def late(i, carry):
            e = h + i
            b = own_ab[1, i]
            a = b
            for k in range(MF):
                a = a + c2o[k] * vg[k, e, own_c]
            own_ab[0, i] = a
            return carry

        loop(nx, late)
        give(0, lambda c: c.start())

        def carry_on(i, past):
            a, b = own_ab[0, i], own_ab[1, i]
            for p in prods:
                value = d_l[p] * past[p] + keep_f[p] * (a + d_f[p] * b)
                y_out[p, i] = value
                out[0, 1 + p, i] = value

        for p in prods:
            up_copy(p, True).wait_recv()

        @pl.when(tm == 1)
        def _():
            for f in range(2):
                up_copy(prony + f, True).wait_recv()

            def body(i, carry):
                u1, u2 = first_in[1, i], first_in[0, i]
                past = [
                    d_l[p] * y_in[p, i] + keep_f[p] * (u2 + d_f[p] * u1) for p in prods
                ]
                carry_on(i, past)
                return carry

            loop(nx, body)

        @pl.when(tm > 1)
        def _():
            def body(i, carry):
                carry_on(i, [y_in[p, i] for p in prods])
                return carry

            loop(nx, body)

        @pl.when(tm < n_tm - 1)
        def _():
            for p in prods:
                up_copy(p, False).start()

        for n in range(1, n_tm):

            @pl.when(tm == n)
            def _():
                for j in range(1, n):
                    for copy in z_copies(j, n):
                        copy.wait_recv()

                def before(i, carry):
                    for p in prods:
                        past = gu_in[0, i]
                        for j in range(2, n):
                            past = d_l[p] * past + gu_in[j - 1, i]
                        out[0, 1 + p, i] = out[0, 1 + p, i] + (d_l[p] * keep_l[p]) * past
                    return carry

                if n > 1:
                    loop(nx, before)
                for copy, (item, at) in zip(z_copies(n, n), z_items(n)):
                    copy.wait_recv()

                    def final_out(t, carry):
                        i = at.start + t
                        u = gu_in[n - 1, i]
                        out[0, 0, i] = u + own_ab[0, i]
                        for p in prods:
                            out[0, 1 + p, i] = out[0, 1 + p, i] + keep_l[p] * u
                        return carry

                    loop(at.size, final_out)

        @pl.when(tm < n_tm - 1)
        def _():
            for p in prods:
                up_copy(p, False).wait_send()

        red_drain(R_COARSE)
        heat_copy().wait_send()
        halo_drain(m_hc)
        for f in range(2):
            give(f, lambda c: c.wait_send())

    halo_drain(m_lab, m_u0, m_h1, m_hd, *m_xf)
    red_drain(R_FINE1)
    red_drain(R_FINE2)


def on_device(sizes, state, labels, rigidity, mismatch, heat, coefs, times):
    _, fields, nx, ny, nz = state.shape
    n_tm = sizes[0]
    stages = n_tm - 1
    inner = max(stages - 1, 1)
    prony = fields - 1
    rows, wide = nx + 2 * RIM + 2, ny + 2 * PAD
    peers = sizes[1] * sizes[2]
    field = (rows, wide, nz)
    own = (nx, ny, nz)
    vmem = pl.BlockSpec(memory_space=pltpu.VMEM)
    smem = pl.BlockSpec(memory_space=pltpu.SMEM)
    dma = pltpu.SemaphoreType.DMA
    reds = R_STAGE + stages
    messages = HIST + prony + 2 * MF + (ML + 2) * inner
    items = stages - 1 + len(chunks_of(nx))

    def vm(*shape):
        return pltpu.VMEM(shape, F32)

    return pl.pallas_call(
        functools.partial(kernel, sizes),
        out_shape=jax.ShapeDtypeStruct(state.shape, state.dtype),
        in_specs=[vmem, vmem, smem, smem, smem, smem, smem],
        out_specs=vmem,
        scratch_shapes=[pltpu.VMEM(field, jnp.int32), vm(4 + prony, *field)]
        + [vm(*field) for _ in range(10)]
        + [
            vm(MF + 1, *field),
            vm(MF + 1, *field),
            vm(ML + 1, *field),
            vm((ML + 1) * stages, *field),
            vm(MF, *field),
            vm(MF, *field),
            vm(ML * inner, *field),
            vm(2 * inner, *field),
            vm(*field),
            vm(*field),
            vm(*field),
            vm(*field),
            vm(prony, *field),
            vm(2, *own),
            vm(stages, *own),
            vm(stages, *own),
            vm(prony, *own),
            vm(prony, *own),
            vm(2, *own),
            vm(stages, 8, nz),
            vm(stages, 8, nz),
            vm(reds, 8, nz),
            vm(reds, max(peers - 1, 1), 8, nz),
            dma((messages, 9)),
            dma((messages, 9)),
            dma((reds,)),
            dma((reds,)),
            dma((stages, items)),
            dma((items,)),
            dma((prony + 2,)),
            dma((prony + 2,)),
            dma,
            dma,
            pltpu.SemaphoreType.REGULAR,
        ],
        compiler_params=pltpu.CompilerParams(
            collective_id=0, has_side_effects=True, vmem_limit_bytes=56 * 1024 * 1024
        ),
    )(state, labels, rigidity, mismatch, heat, coefs, times)


def solution(mesh):
    sizes = tuple(mesh.shape[name] for name in ("tm", "gx", "gy"))
    placed = (
        P("tm", None, "gx", "gy", None),
        P("gx", "gy", None),
        P(),
        P(),
        P("tm", None),
        P(),
        P(),
    )
    return jax.shard_map(
        functools.partial(on_device, sizes),
        mesh=mesh,
        in_specs=placed,
        out_specs=P("tm", None, "gx", "gy", None),
        check_vma=False,
    )
```
